32 devices in a mesh: dp: 4 (over y, core), expert: 8 (over z, x).
Axes of the slice: x: 2, y: 2, z: 4, core: 2. Of those that a mesh axis runs over, the one named last changes fastest.
Arguments:
- tokens: bfloat16 [4, 1024, 4096], P('dp', 'expert'), may hold values from -20 to 20
- router_weight: bfloat16 [4096, 128], replicated
- chosen: int32 [4, 1, 128], P('dp'), may hold values from 0 to 1023, as said below
- w_gate: bfloat16 [4096, 1536], P(None, 'expert'), may hold values from -0.09375 to 0.09375
- w_up: bfloat16 [4096, 1536], P(None, 'expert'), may hold values from -0.09375 to 0.09375
- w_down: bfloat16 [1536, 4096], P('expert'), may hold values from -0.15625 to 0.15625
Outputs:
- combined: bfloat16 [4, 1024, 4096], P('dp', 'expert')
- z_loss: float32 [], replicated
The draws below stay inside these ranges and needn't reach their ends.
Inputs may be any that keep to these rules, and one draw needn't show every extreme that they name: Each list chosen[g, e] holds 128 distinct positions of window g; at most 32 of them lie in any one aligned block of 128 positions (the tokens of one device), and some block holds exactly 32.
All inputs are finite; a program needn't handle non-finite values.
Results may differ from the reference program's by a relative error of at most 0.009.
Values may be sent and summed in bfloat16 or wider, within the bound.
A program may use at most 64 MiB of HBM per device.

```python
import jax
import jax.numpy as jnp
from jax import lax

D = 4096
FF = 1536
NE = 128
TOK_DEV = 128
CAP = 128
SPLIT = 8
EXPERTS = 1
TOKENS = 1024
MOST = 32
N_DP = 4
N_EXPERT = 8


def chosen_layout(key):
    base = jax.random.fold_in(key, 7001)
    quarter = N_EXPERT // 4
    pattern = jnp.concatenate([jnp.full((quarter,), MOST, jnp.int32), jnp.full((2 * quarter,), MOST // 2, jnp.int32), jnp.zeros((N_EXPERT - 3 * quarter,), jnp.int32)])

    def one_list(group, expert):
        shared = jnp.where(expert == 1, 0, expert)
        group_key = jax.random.fold_in(base, group)
        count_key = jax.random.fold_in(jax.random.fold_in(group_key, 1), shared)
        token_key = jax.random.fold_in(jax.random.fold_in(group_key, 2), shared)
        counts = pattern[jax.random.permutation(count_key, N_EXPERT)]
        counts = jnp.where(expert == 1, jnp.roll(counts, 1), counts)
        orders = jax.vmap(lambda subkey: jax.random.permutation(subkey, TOK_DEV))(jax.random.split(token_key, N_EXPERT))
        orders = orders.astype(jnp.int32)
        owners = jnp.arange(N_EXPERT, dtype=jnp.int32)[:, None] * TOK_DEV
        candidates = (owners + orders[:, :MOST]).reshape(-1)
        live = (jnp.arange(MOST, dtype=jnp.int32)[None, :] < counts[:, None]).reshape(-1)
        ranking = jnp.where(live, 0, 1) * (N_EXPERT * MOST) + jnp.arange(N_EXPERT * MOST, dtype=jnp.int32)
        placing = jnp.argsort(ranking, stable=True)
        return (candidates[placing[:CAP]].astype(jnp.int32), counts, orders[:, 0])
    groups = jnp.arange(N_DP, dtype=jnp.int32)
    experts_all = jnp.arange(EXPERTS, dtype=jnp.int32)
    lists, counts, firsts = jax.vmap(lambda group: jax.vmap(lambda expert: one_list(group, expert))(experts_all))(groups)
    second = 1 if EXPERTS > 1 else 0
    shared_live = ((counts[:, 0] > 0) & (counts[:, second] > 0)).astype(jnp.int32)
    source = jnp.argmax(shared_live, axis=1).astype(jnp.int32)
    aligned = source * TOK_DEV + jnp.take_along_axis(firsts[:, 0], source[:, None], axis=1)[:, 0]
    return (lists, aligned.astype(jnp.int32))


def drawn_vectors(key):
    return jax.random.truncated_normal(jax.random.fold_in(key, 7301), -4.0, 4.0, (N_DP, D), jnp.float32)


def draw_chosen(key, part):
    return chosen_layout(key)[0]


def draw_tokens(key, part):
    lists, aligned = chosen_layout(key)
    value_key = jax.random.fold_in(key, 7101)
    factor_key = jax.random.fold_in(key, 7102)
    position = jnp.arange(N_DP, dtype=jnp.float32)[:, None] * TOKENS + jnp.arange(TOKENS, dtype=jnp.float32)[None, :]
    fraction = position / max(N_DP * TOKENS - 1, 1)
    values = jax.random.truncated_normal(value_key, -4.0, 4.0, (N_DP, TOKENS, D), jnp.float32)
    scale = 0.6 * 5.0 ** fraction
    factor = jnp.exp(jax.random.uniform(factor_key, (N_DP, TOKENS), jnp.float32, -0.35, 0.35))
    values = values * (scale * factor)[:, :, None]
    values = values.at[jnp.arange(N_DP), aligned].set(drawn_vectors(key))
    return values.astype(jnp.bfloat16)


def draw_router_weight(key, part):
    weights = jax.random.truncated_normal(jax.random.fold_in(key, 7201), -4.0, 4.0, (D, NE), jnp.float32) / jnp.sqrt(float(D))
    return weights.astype(jnp.bfloat16)


def block_levels(rng, extent, shards, least, largest):
    level, own = 1.0, jax.random.fold_in(rng, 6)
    for dim, blocks in shards:
        draws = jnp.exp(jax.random.uniform(jax.random.fold_in(own, dim), (blocks,), jnp.float32, least / len(shards), largest / len(shards)))
        level = level * jnp.repeat(draws, extent[dim] // blocks).reshape([-1 if axis == dim else 1 for axis in range(len(extent))])
    return level


def normal_values(rng, shape, deviation, bound, pieces=(), kind=jnp.bfloat16):
    result = deviation * jax.random.normal(rng, shape, jnp.float32)
    if pieces:
        result = result * block_levels(rng, shape, pieces, -0.22, 0.18)
    return jnp.clip(result, -bound, bound).astype(kind)


def setup_inputs(seed: int = 0) -> dict:
    keys = jax.random.split(jax.random.key(seed), 7)
    return {
        "tokens": draw_tokens(jax.random.fold_in(keys[6], 71), 0),
        "router_weight": draw_router_weight(jax.random.fold_in(keys[6], 71), 0),
        "chosen": draw_chosen(jax.random.fold_in(keys[6], 71), 0),
        "w_gate": normal_values(keys[3], (D, EXPERTS * FF), D ** -0.5, 0.09375, ((1, 8),)),
        "w_up": normal_values(keys[4], (D, EXPERTS * FF), D ** -0.5, 0.09375, ((1, 8),)),
        "w_down": normal_values(keys[5], (EXPERTS * FF, D), FF ** -0.5, 0.15625, ((0, 8),)),
    }


def one_window(token_rows, picked, router_weight, w_gate, w_up, w_down):
    logits = jnp.dot(token_rows, router_weight, preferred_element_type=jnp.float32)
    highest = jnp.max(logits, axis=1, keepdims=True)
    log_total = highest[:, 0] + jnp.log(jnp.sum(jnp.exp(logits - highest), axis=1))
    loss_part = jnp.sum(log_total * log_total)
    expert_ids = jnp.arange(EXPERTS, dtype=jnp.int32)
    member = jnp.zeros((TOKENS, EXPERTS), jnp.float32).at[picked, expert_ids[:, None]].set(1.0) > 0.5
    window = logits[:, :EXPERTS]
    peak = jnp.max(jnp.where(member, window, -1e30), axis=1, keepdims=True)
    peak = jnp.where(jnp.any(member, axis=1, keepdims=True), peak, 0.0)
    raised = jnp.where(member, jnp.exp(jnp.where(member, window - peak, -60.0)), 0.0)
    denom = jnp.sum(raised, axis=1, keepdims=True)
    combine = raised / jnp.where(denom > 0, denom, 1.0)
    slice_width = FF // SPLIT

    def expert_step(mixed, expert):
        rows = token_rows[picked[expert]]
        start = (expert * FF).astype(jnp.int32)
        gate_cols = lax.dynamic_slice_in_dim(w_gate, start, FF, 1)
        up_cols = lax.dynamic_slice_in_dim(w_up, start, FF, 1)
        down_rows = lax.dynamic_slice_in_dim(w_down, start, FF, 0)
        gate = jnp.dot(rows, gate_cols, preferred_element_type=jnp.float32)
        upper = jnp.dot(rows, up_cols, preferred_element_type=jnp.float32)
        hidden = (jax.nn.silu(gate) * upper).astype(jnp.bfloat16)
        summed = jnp.zeros((CAP, D), jnp.float32)
        for piece_no in range(SPLIT):
            lower = piece_no * slice_width
            part = jnp.dot(hidden[:, lower:lower + slice_width], down_rows[lower:lower + slice_width], preferred_element_type=jnp.float32)
            part = lax.optimization_barrier(part.astype(jnp.bfloat16))
            summed = summed + part.astype(jnp.float32)
        expert_out = summed.astype(jnp.bfloat16)
        scale = combine[picked[expert], expert]
        mixed = mixed.at[picked[expert]].add(scale[:, None] * expert_out.astype(jnp.float32))
        return mixed, None

    mixed, _ = lax.scan(expert_step, jnp.zeros((TOKENS, D), jnp.float32), expert_ids)
    return mixed.astype(jnp.bfloat16), loss_part


def reference(tokens, router_weight, chosen, w_gate, w_up, w_down):
    def window_fn(pair):
        return one_window(pair[0], pair[1], router_weight, w_gate, w_up, w_down)

    combined, loss_parts = lax.map(window_fn, (tokens, chosen))
    z_loss = jnp.sum(loss_parts) / (N_DP * TOKENS)
    return combined, z_loss
```

```python
import functools

import jax
import jax.numpy as jnp
from jax import lax
from jax.experimental import pallas as pl
from jax.experimental.pallas import tpu as pltpu
from jax.sharding import PartitionSpec as P

MESH = pl.DeviceIdType.MESH
F32 = jnp.float32
BF16 = jnp.bfloat16


def flip(index, mask):
    result = index
    bit = 0
    while mask >> bit:
        if mask >> bit & 1:
            result = result + 2**bit * (1 - 2 * (index // 2**bit % 2))
        bit += 1
    return result


class Tree:
    def __init__(self, levels, order):
        self.blocks = 2**levels
        self.bit = {}
        for j in range(1, self.blocks):
            self.bit[j] = [b for b in order if j >> b & 1][-1]
        self.parent = {j: j ^ 1 << b for j, b in self.bit.items()}
        self.children = [
            sorted((j for j in self.parent if self.parent[j] == i), key=lambda j: order.index(self.bit[j]))
            for i in range(self.blocks)
        ]
        self.depth = [bin(j).count("1") for j in range(self.blocks)]
        self.height = [self._height(j) for j in range(self.blocks)]

    def _height(self, j):
        return 1 + max(self._height(i) for i in self.children[j]) if self.children[j] else 0


def kernel(cfg, *refs):
    groups, split, most, dp_bits, ex_bits, trees, chunk, tokens_all = cfg
    (tok_h, rw_h, chosen_ref, wg_h, wu_h, wd_h, out_ref, z_ref,
     tok, rw, wg, wu, wd, rows_x, send_y, recv_y, part_y, z_acc, z_in,
     local_sem, ag_send, ag_recv, rs_send, rs_recv, z_send, z_recv) = refs[:26]
    levels = split.bit_length() - 1
    me = lax.axis_index("expert")
    me_dp = lax.axis_index("dp")
    my_group = me // split
    rows_dev, width = tok.shape
    cap = chosen_ref.shape[1]
    block = groups * most
    chunks = len(trees)

    local = [
        pltpu.make_async_copy(src, dst, local_sem.at[i])
        for i, (src, dst) in enumerate(((tok_h, tok), (wg_h, wg), (wu_h, wu), (rw_h, rw), (wd_h, wd)))
    ]
    for copy in local:
        copy.start()

    ex_masks = [1 << b for b in range(levels)] + [split * k for k in range(1, groups)]
    partners = [{"expert": flip(me, mask)} for mask in ex_masks]
    partners += [{"dp": flip(me_dp, 1 << b)} for b in range(dp_bits)]
    barrier = pltpu.get_barrier_semaphore()
    for partner in partners:
        pl.semaphore_signal(barrier, inc=1, device_id=partner, device_id_type=MESH)

    t_sub = lax.broadcasted_iota(jnp.int32, (rows_dev, cap), 0)
    sq_row = lax.broadcasted_iota(jnp.int32, (rows_dev, rows_dev), 0)
    sq_col = lax.broadcasted_iota(jnp.int32, (rows_dev, rows_dev), 1)
    before = (sq_row < sq_col).astype(F32).astype(BF16)
    after = (sq_col < sq_row).astype(F32).astype(BF16)
    slot_sub = lax.broadcasted_iota(jnp.int32, (most, rows_dev), 0).astype(F32)
    slot_lane = lax.broadcasted_iota(jnp.int32, (rows_dev, most), 1).astype(F32)
    picks, places, members = [], [], []
    for k in range(groups):
        row = chosen_ref[pl.ds(flip(my_group, k), 1), :] - me * rows_dev
        equal = (row == t_sub).astype(F32)
        member = jnp.max(equal, axis=1, keepdims=True)
        ones = jnp.ones((8, cap), BF16)
        member_row = lax.dot_general(ones, equal.astype(BF16), (((1,), (1,)), ((), ())), preferred_element_type=F32)
        rank_row = jnp.dot(member_row.astype(BF16), before, preferred_element_type=F32)
        pick = jnp.where(member_row[0:1] > 0.5, (rank_row[0:1] == slot_sub).astype(F32), 0.0)
        wide = jnp.broadcast_to(member, (rows_dev, most))
        rank_col = jnp.dot(after, wide.astype(BF16), preferred_element_type=F32)
        place = jnp.where(wide > 0.5, (rank_col == slot_lane).astype(F32), 0.0)
        picks.append(pick.astype(BF16))
        places.append(place.astype(BF16))
        members.append(member)

    def cols(c):
        return pl.ds(c * chunk, chunk)

    def ag_copy(c, j):
        tree = trees[c]
        return pltpu.make_async_remote_copy(
            src_ref=rows_x.at[tree.parent[j], :, cols(c)],
            dst_ref=rows_x.at[j, :, cols(c)],
            send_sem=ag_send.at[c, j],
            recv_sem=ag_recv.at[c, j],
            device_id={"expert": flip(me, 1 << tree.bit[j])},
            device_id_type=MESH,
        )

    def rs_copy(c, j):
        tree = trees[c]
        return pltpu.make_async_remote_copy(
            src_ref=send_y.at[j, :, cols(c)],
            dst_ref=recv_y.at[j, :, cols(c)],
            send_sem=rs_send.at[c, j],
            recv_sem=rs_recv.at[c, j],
            device_id={"expert": flip(me, 1 << tree.bit[j])},
            device_id_type=MESH,
        )

    z_steps = [("expert", flip(me, 1 << b)) for b in range(ex_bits)]
    z_steps += [("dp", flip(me_dp, 1 << b)) for b in range(dp_bits)]

    def z_copy(s):
        axis, partner = z_steps[s]
        return pltpu.make_async_remote_copy(
            src_ref=z_acc.at[s],
            dst_ref=z_in.at[s],
            send_sem=z_send.at[s],
            recv_sem=z_recv.at[s],
            device_id={axis: partner},
            device_id_type=MESH,
        )

    def z_advance(s):
        if s > 0:
            z_copy(s - 1).wait()
            z_acc[s] = z_acc[s - 1] + z_in[s - 1]
        if s < len(z_steps):
            z_copy(s).start()

    pl.semaphore_wait(barrier, len(partners))
    local[0].wait()
    if groups == 1:
        for c in range(chunks):
            rows_x[0, :, cols(c)] = jnp.dot(picks[0], tok[:, cols(c)], preferred_element_type=F32).astype(BF16)
            for j in trees[c].children[0]:
                ag_copy(c, j).start()
    else:
        slots, stage, back_out, back_in, ex_send, ex_recv, bk_send, bk_recv = refs[26:]

        def across(k, src, dst, send, recv):
            return pltpu.make_async_remote_copy(
                src_ref=src.at[k],
                dst_ref=dst.at[k],
                send_sem=send.at[k],
                recv_sem=recv.at[k],
                device_id={"expert": flip(me, split * k)},
                device_id_type=MESH,
            )

        def spread(k):
            sub = lax.broadcasted_iota(jnp.int32, (block, most), 0)
            lane = lax.broadcasted_iota(jnp.int32, (block, most), 1)
            return (sub == lane + k * most).astype(F32).astype(BF16)

        def collect(k):
            sub = lax.broadcasted_iota(jnp.int32, (most, block), 0)
            lane = lax.broadcasted_iota(jnp.int32, (most, block), 1)
            return (lane == sub + k * most).astype(F32).astype(BF16)

        for k in range(groups):
            for c in range(chunks):
                slots[k, :, cols(c)] = jnp.dot(picks[k], tok[:, cols(c)], preferred_element_type=F32).astype(BF16)
            if k:
                across(k, slots, stage, ex_send, ex_recv).start()
        for k in range(1, groups):
            across(k, slots, stage, ex_send, ex_recv).wait()
        for c in range(chunks):
            total = jnp.dot(spread(0), slots[0, :, cols(c)], preferred_element_type=F32)
            for k in range(1, groups):
                total = total + jnp.dot(spread(k), stage[k, :, cols(c)], preferred_element_type=F32)
            rows_x[0, :, cols(c)] = total.astype(BF16)
            for j in trees[c].children[0]:
                ag_copy(c, j).start()

    local[3].wait()
    logits = jnp.dot(tok[...], rw[...], preferred_element_type=F32)
    highest = jnp.max(logits, axis=1, keepdims=True)
    log_total = highest + jnp.log(jnp.sum(jnp.exp(logits - highest), axis=1, keepdims=True))
    z_part = jnp.sum(log_total * log_total, axis=0, keepdims=True)
    z_acc[0] = jnp.broadcast_to(z_part, z_acc.shape[1:])
    lane = lax.broadcasted_iota(jnp.int32, logits.shape, 1)
    window = [
        jnp.sum(jnp.where(lane == flip(my_group, k), logits, 0.0), axis=1, keepdims=True) for k in range(groups)
    ]
    peak = jnp.where(members[0] > 0.5, window[0], -1e30)
    some = members[0]
    for k in range(1, groups):
        peak = jnp.maximum(peak, jnp.where(members[k] > 0.5, window[k], -1e30))
        some = jnp.maximum(some, members[k])
    peak = jnp.where(some > 0.5, peak, 0.0)
    raised = [
        jnp.where(members[k] > 0.5, jnp.exp(jnp.where(members[k] > 0.5, window[k] - peak, -60.0)), 0.0)
        for k in range(groups)
    ]
    denom = functools.reduce(lambda a, b: a + b, raised)
    weights = [value / jnp.where(denom > 0, denom, 1.0) for value in raised]

    local[1].wait()
    local[2].wait()
    gate = jnp.zeros((split * block, wg.shape[1]), F32)
    upper = jnp.zeros((split * block, wg.shape[1]), F32)
    z_done = 0
    for t in range(chunks + levels - 1):
        for depth in range(levels, 0, -1):
            c = t - (depth - 1)
            if 0 <= c < chunks:
                for j in range(split):
                    if trees[c].depth[j] == depth:
                        ag_copy(c, j).wait_recv()
                        for i in trees[c].children[j]:
                            ag_copy(c, i).start()
        if z_done <= len(z_steps):
            z_advance(z_done)
            z_done += 1
        c = t - (levels - 1)
        if c >= 0:
            rows = rows_x[:, :, cols(c)].reshape(split * block, chunk)
            gate = gate + jnp.dot(rows, wg[cols(c), :], preferred_element_type=F32)
            upper = upper + jnp.dot(rows, wu[cols(c), :], preferred_element_type=F32)
    hidden = (gate / (1.0 + jnp.exp(-gate)) * upper).astype(BF16)

    local[4].wait()
    for c in range(chunks):
        part = jnp.dot(hidden, wd[:, cols(c)], preferred_element_type=F32)
        for j in range(split):
            piece = part[j * block:(j + 1) * block]
            if trees[c].height[j] == 0:
                send_y[j, :, cols(c)] = piece.astype(BF16)
                rs_copy(c, j).start()
            else:
                part_y[j, :, cols(c)] = piece

    while z_done <= len(z_steps):
        z_advance(z_done)
        z_done += 1
    z_ref[...] = z_acc[len(z_steps)][0:1, 0:1] / tokens_all

    def mix(c, rows_of):
        mixed = weights[0] * jnp.dot(places[0], rows_of(0), preferred_element_type=F32)
        for k in range(1, groups):
            mixed = mixed + weights[k] * jnp.dot(places[k], rows_of(k), preferred_element_type=F32)
        out_ref[:, cols(c)] = mixed.astype(out_ref.dtype)

    tallest = trees[0].height[0]
    for t in range(chunks + tallest - 1):
        for height in range(tallest, 0, -1):
            c = t - (height - 1)
            if not 0 <= c < chunks:
                continue
            for j in range(split):
                if trees[c].height[j] != height:
                    continue
                total = part_y[j, :, cols(c)]
                for i in reversed(trees[c].children[j]):
                    rs_copy(c, i).wait_recv()
                    total = total + recv_y[i, :, cols(c)].astype(F32)
                if j:
                    send_y[j, :, cols(c)] = total.astype(BF16)
                    rs_copy(c, j).start()
                elif groups == 1:
                    done = total.astype(BF16)
                    mix(c, lambda k: done)
                else:
                    send_y[0, :, cols(c)] = total.astype(BF16)

    if groups > 1:
        for k in range(groups):
            for c in range(chunks):
                piece = jnp.dot(collect(k), send_y[0, :, cols(c)], preferred_element_type=F32).astype(BF16)
                back_out[k, :, cols(c)] = piece
            if k:
                across(k, back_out, back_in, bk_send, bk_recv).start()
        for k in range(1, groups):
            across(k, back_out, back_in, bk_send, bk_recv).wait()
        for c in range(chunks):
            mix(c, lambda k: (back_in if k else back_out)[k, :, cols(c)])

    for c in range(chunks):
        for j in range(1, split):
            ag_copy(c, j).wait_send()
            rs_copy(c, j).wait_send()


def body(ex_size, dp_size, tokens, router_weight, chosen, w_gate, w_up, w_down):
    token_rows, picked = tokens[0], chosen[0]
    groups, cap = picked.shape
    rows_dev, width = token_rows.shape
    split = ex_size // groups
    levels = split.bit_length() - 1
    most = 2 * cap // ex_size
    block = groups * most
    ex_bits = ex_size.bit_length() - 1
    dp_bits = dp_size.bit_length() - 1
    chunks = max(1, width // 512)
    chunk = width // chunks
    plain = tuple(range(levels - 1, -1, -1))
    swapped = plain[:-2] + plain[:-3:-1]
    trees = [Tree(levels, swapped if c % 4 == 1 else plain) for c in range(chunks)]
    cfg = (groups, split, most, dp_bits, ex_bits, trees, chunk, float(dp_size * ex_size * rows_dev))
    z_slots = ex_bits + dp_bits + 1
    hidden = w_gate.shape[1]
    dma = pltpu.SemaphoreType.DMA
    scratch = [
        pltpu.VMEM((rows_dev, width), BF16),
        pltpu.VMEM(router_weight.shape, BF16),
        pltpu.VMEM((width, hidden), BF16),
        pltpu.VMEM((width, hidden), BF16),
        pltpu.VMEM((hidden, width), BF16),
        pltpu.VMEM((split, block, width), BF16),
        pltpu.VMEM((split, block, width), BF16),
        pltpu.VMEM((split, block, width), BF16),
        pltpu.VMEM((split, block, width), F32),
        pltpu.VMEM((z_slots, 8, 128), F32),
        pltpu.VMEM((z_slots, 8, 128), F32),
        dma((5,)),
        dma((chunks, split)),
        dma((chunks, split)),
        dma((chunks, split)),
        dma((chunks, split)),
        dma((z_slots,)),
        dma((z_slots,)),
    ]
    if groups > 1:
        scratch += [pltpu.VMEM((groups, most, width), BF16)] * 4 + [dma((groups,))] * 4
    any_spec = pl.BlockSpec(memory_space=pl.ANY)
    vmem_spec = pl.BlockSpec(memory_space=pltpu.VMEM)
    combined, z_loss = pl.pallas_call(
        functools.partial(kernel, cfg),
        out_shape=(
            jax.ShapeDtypeStruct((rows_dev, width), BF16),
            jax.ShapeDtypeStruct((1, 1), F32),
        ),
        in_specs=[any_spec, any_spec, vmem_spec, any_spec, any_spec, any_spec],
        out_specs=(vmem_spec, vmem_spec),
        scratch_shapes=scratch,
        compiler_params=pltpu.CompilerParams(collective_id=0, has_side_effects=True),
    )(token_rows, router_weight, picked, w_gate, w_up, w_down)
    return combined[None], z_loss.reshape(())


def solution(mesh):
    in_specs = (
        P("dp", "expert", None),
        P(),
        P("dp", None, None),
        P(None, "expert"),
        P(None, "expert"),
        P("expert", None),
    )
    out_specs = (P("dp", "expert", None), P())
    step = functools.partial(body, mesh.shape["expert"], mesh.shape["dp"])
    return jax.shard_map(step, mesh=mesh, in_specs=in_specs, out_specs=out_specs, check_vma=False)
```

```python
import functools

import jax
import jax.numpy as jnp
from jax import lax
from jax.experimental import pallas as pl
from jax.experimental.pallas import tpu as pltpu
from jax.sharding import PartitionSpec as P

MESH = pl.DeviceIdType.MESH
F32 = jnp.float32
BF16 = jnp.bfloat16
LAG = 1


def flip(index, mask):
    result = index
    bit = 0
    while mask >> bit:
        if mask >> bit & 1:
            result = result + 2**bit * (1 - 2 * (index // 2**bit % 2))
        bit += 1
    return result


def times_t(a, b):
    return lax.dot_general(a, b, (((1,), (1,)), ((), ())), preferred_element_type=F32)


def source(j):
    return j - 1 if j % 2 else 0


def kernel(cfg, *refs):
    groups, split, most, dp_bits, ex_bits, chunks, chunk, tokens_all = cfg
    (tok_h, rw_h, chosen_ref, wg_h, wu_h, wd_h, out_ref, z_ref,
     tok, rw, wg, wu, wd, rows_x, send_y, recv_y, part_y, z_acc, z_in,
     local_sem, ag_send, ag_recv, rs_send, rs_recv, z_send, z_recv) = refs[:26]
    me = lax.axis_index("expert")
    me_dp = lax.axis_index("dp")
    my_group = me // split
    rows_dev, width = tok.shape
    cap = chosen_ref.shape[1]
    block = groups * most

    local = [
        pltpu.make_async_copy(src, dst, local_sem.at[i])
        for i, (src, dst) in enumerate(((tok_h, tok), (wg_h, wg), (wu_h, wu), (rw_h, rw), (wd_h, wd)))
    ]
    for copy in local:
        copy.start()

    ex_masks = [1] + list(range(2, split, 2)) + [split * k for k in range(1, groups)]
    partners = [{"expert": flip(me, mask)} for mask in ex_masks]
    partners += [{"dp": flip(me_dp, 1 << b)} for b in range(dp_bits)]
    barrier = pltpu.get_barrier_semaphore()
    for partner in partners:
        pl.semaphore_signal(barrier, inc=1, device_id=partner, device_id_type=MESH)

    t_sub = lax.broadcasted_iota(jnp.int32, (rows_dev, cap), 0)
    sq_row = lax.broadcasted_iota(jnp.int32, (rows_dev, rows_dev), 0)
    sq_col = lax.broadcasted_iota(jnp.int32, (rows_dev, rows_dev), 1)
    before = (sq_row < sq_col).astype(F32).astype(BF16)
    after = (sq_col < sq_row).astype(F32).astype(BF16)
    slot_sub = lax.broadcasted_iota(jnp.int32, (most, rows_dev), 0).astype(F32)
    slot_lane = lax.broadcasted_iota(jnp.int32, (rows_dev, most), 1).astype(F32)
    picks, places, members = [], [], []
    for k in range(groups):
        row = chosen_ref[pl.ds(flip(my_group, k), 1), :] - me * rows_dev
        equal = (row == t_sub).astype(F32)
        member = jnp.max(equal, axis=1, keepdims=True)
        ones = jnp.ones((8, cap), BF16)
        member_row = times_t(ones, equal.astype(BF16))
        rank_row = jnp.dot(member_row.astype(BF16), before, preferred_element_type=F32)
        pick = jnp.where(member_row[0:1] > 0.5, (rank_row[0:1] == slot_sub).astype(F32), 0.0)
        wide = jnp.broadcast_to(member, (rows_dev, most))
        rank_col = jnp.dot(after, wide.astype(BF16), preferred_element_type=F32)
        place = jnp.where(wide > 0.5, (rank_col == slot_lane).astype(F32), 0.0)
        picks.append(pick.astype(BF16))
        places.append(place.astype(BF16))
        members.append(member)

    def cols(c):
        return pl.ds(c * chunk, chunk)

    def ag_copy(c, j):
        return pltpu.make_async_remote_copy(
            src_ref=rows_x.at[c, source(j)],
            dst_ref=rows_x.at[c, j],
            send_sem=ag_send.at[c, j],
            recv_sem=ag_recv.at[c, j],
            device_id={"expert": flip(me, j - source(j))},
            device_id_type=MESH,
        )

    def rs_copy(c, j):
        return pltpu.make_async_remote_copy(
            src_ref=send_y.at[c, j],
            dst_ref=recv_y.at[c, j],
            send_sem=rs_send.at[c, j],
            recv_sem=rs_recv.at[c, j],
            device_id={"expert": flip(me, j - source(j))},
            device_id_type=MESH,
        )

    far = [j for j in range(split - 2, 0, -2)]

    z_steps = [("expert", flip(me, 1 << b)) for b in range(ex_bits)]
    z_steps += [("dp", flip(me_dp, 1 << b)) for b in range(dp_bits)]

    def z_copy(s):
        axis, partner = z_steps[s]
        return pltpu.make_async_remote_copy(
            src_ref=z_acc.at[s],
            dst_ref=z_in.at[s],
            send_sem=z_send.at[s],
            recv_sem=z_recv.at[s],
            device_id={axis: partner},
            device_id_type=MESH,
        )

    def z_advance(s):
        if s > 0:
            z_copy(s - 1).wait()
            z_acc[s] = z_acc[s - 1] + z_in[s - 1]
        if s < len(z_steps):
            z_copy(s).start()

    pl.semaphore_wait(barrier, len(partners))
    local[0].wait()
    if groups == 1:
        for c in range(chunks):
            rows_x[c, 0] = jnp.dot(picks[0], tok[:, cols(c)], preferred_element_type=F32).astype(BF16)
            for j in far + [1]:
                ag_copy(c, j).start()
    else:
        slots, stage, back_out, back_in, ex_send, ex_recv, bk_send, bk_recv = refs[26:]

        def across(k, src, dst, send, recv):
            return pltpu.make_async_remote_copy(
                src_ref=src.at[k],
                dst_ref=dst.at[k],
                send_sem=send.at[k],
                recv_sem=recv.at[k],
                device_id={"expert": flip(me, split * k)},
                device_id_type=MESH,
            )

        def spread(k):
            sub = lax.broadcasted_iota(jnp.int32, (block, most), 0)
            lane = lax.broadcasted_iota(jnp.int32, (block, most), 1)
            return (sub == lane + k * most).astype(F32).astype(BF16)

        def collect(k):
            sub = lax.broadcasted_iota(jnp.int32, (most, block), 0)
            lane = lax.broadcasted_iota(jnp.int32, (most, block), 1)
            return (lane == sub + k * most).astype(F32).astype(BF16)

        for k in range(groups):
            for c in range(chunks):
                slots[k, :, cols(c)] = jnp.dot(picks[k], tok[:, cols(c)], preferred_element_type=F32).astype(BF16)
            if k:
                across(k, slots, stage, ex_send, ex_recv).start()
        for k in range(1, groups):
            across(k, slots, stage, ex_send, ex_recv).wait()
        for c in range(chunks):
            total = jnp.dot(spread(0), slots[0, :, cols(c)], preferred_element_type=F32)
            for k in range(1, groups):
                total = total + jnp.dot(spread(k), stage[k, :, cols(c)], preferred_element_type=F32)
            rows_x[c, 0] = total.astype(BF16)
            for j in far + [1]:
                ag_copy(c, j).start()

    local[3].wait()
    logits = jnp.dot(tok[...], rw[...], preferred_element_type=F32)
    highest = jnp.max(logits, axis=1, keepdims=True)
    log_total = highest + jnp.log(jnp.sum(jnp.exp(logits - highest), axis=1, keepdims=True))
    z_part = jnp.sum(log_total * log_total, axis=0, keepdims=True)
    z_acc[0] = jnp.broadcast_to(z_part, z_acc.shape[1:])
    lane = lax.broadcasted_iota(jnp.int32, logits.shape, 1)
    window = [
        jnp.sum(jnp.where(lane == flip(my_group, k), logits, 0.0), axis=1, keepdims=True) for k in range(groups)
    ]
    peak = jnp.where(members[0] > 0.5, window[0], -1e30)
    some = members[0]
    for k in range(1, groups):
        peak = jnp.maximum(peak, jnp.where(members[k] > 0.5, window[k], -1e30))
        some = jnp.maximum(some, members[k])
    peak = jnp.where(some > 0.5, peak, 0.0)
    raised = [
        jnp.where(members[k] > 0.5, jnp.exp(jnp.where(members[k] > 0.5, window[k] - peak, -60.0)), 0.0)
        for k in range(groups)
    ]
    denom = functools.reduce(lambda a, b: a + b, raised)
    weights = [value / jnp.where(denom > 0, denom, 1.0) for value in raised]

    local[1].wait()
    local[2].wait()
    gate = jnp.zeros((split * block, wg.shape[0]), F32)
    upper = jnp.zeros((split * block, wg.shape[0]), F32)
    z_done = 0
    for t in range(chunks + LAG):
        if t < chunks:
            for j in reversed(far):
                ag_copy(t, j).wait_recv()
                ag_copy(t, j + 1).start()
        if z_done <= len(z_steps):
            z_advance(z_done)
            z_done += 1
        c = t - LAG
        if c >= 0:
            for j in range(1, split, 2):
                ag_copy(c, j).wait_recv()
            rows = rows_x[c].reshape(split * block, chunk)
            gate = gate + times_t(rows, wg[:, cols(c)])
            upper = upper + times_t(rows, wu[:, cols(c)])
    hidden = (gate / (1.0 + jnp.exp(-gate)) * upper).astype(BF16)

    local[4].wait()

    def down(c):
        part = jnp.dot(hidden, wd[:, cols(c)], preferred_element_type=F32)
        for j in reversed(range(split)):
            piece = part[j * block:(j + 1) * block]
            if j % 2:
                send_y[c, j] = piece.astype(BF16)
                rs_copy(c, j).start()
            else:
                part_y[c, j // 2] = piece

    for c in range(chunks):
        down(c)

    while z_done <= len(z_steps):
        z_advance(z_done)
        z_done += 1
    z_ref[...] = z_acc[len(z_steps)][0:1, 0:1] / tokens_all

    def mix(c, rows_of):
        mixed = weights[0] * jnp.dot(places[0], rows_of(0), preferred_element_type=F32)
        for k in range(1, groups):
            mixed = mixed + weights[k] * jnp.dot(places[k], rows_of(k), preferred_element_type=F32)
        out_ref[:, cols(c)] = mixed.astype(out_ref.dtype)

    for t in range(chunks + LAG):
        if t < chunks:
            for j in far:
                rs_copy(t, j + 1).wait_recv()
                send_y[t, j] = (part_y[t, j // 2] + recv_y[t, j + 1].astype(F32)).astype(BF16)
                rs_copy(t, j).start()
        c = t - LAG
        if c >= 0:
            total = part_y[c, 0]
            for j in [1] + far:
                rs_copy(c, j).wait_recv()
                total = total + recv_y[c, j].astype(F32)
            done = total.astype(BF16)
            if groups == 1:
                mix(c, lambda k: done)
            else:
                send_y[c, 0] = done

    if groups > 1:
        for k in range(groups):
            for c in range(chunks):
                piece = jnp.dot(collect(k), send_y[c, 0], preferred_element_type=F32).astype(BF16)
                back_out[k, :, cols(c)] = piece
            if k:
                across(k, back_out, back_in, bk_send, bk_recv).start()
        for k in range(1, groups):
            across(k, back_out, back_in, bk_send, bk_recv).wait()
        for c in range(chunks):
            mix(c, lambda k: (back_in if k else back_out)[k, :, cols(c)])

    for c in range(chunks):
        for j in range(1, split):
            ag_copy(c, j).wait_send()
            rs_copy(c, j).wait_send()


def body(ex_size, dp_size, tokens, router_weight, chosen, w_gate, w_up, w_down):
    token_rows, picked = tokens[0], chosen[0]
    groups, cap = picked.shape
    rows_dev, width = token_rows.shape
    split = ex_size // groups
    most = 2 * cap // ex_size
    block = groups * most
    ex_bits = ex_size.bit_length() - 1
    dp_bits = dp_size.bit_length() - 1
    chunks = max(1, width // 1024)
    chunk = width // chunks
    cfg = (groups, split, most, dp_bits, ex_bits, chunks, chunk, float(dp_size * ex_size * rows_dev))
    z_slots = ex_bits + dp_bits + 1
    hidden = w_gate.shape[1]
    dma = pltpu.SemaphoreType.DMA
    scratch = [
        pltpu.VMEM((rows_dev, width), BF16),
        pltpu.VMEM(router_weight.shape, BF16),
        pltpu.VMEM((hidden, width), BF16),
        pltpu.VMEM((hidden, width), BF16),
        pltpu.VMEM((hidden, width), BF16),
        pltpu.VMEM((chunks, split, block, chunk), BF16),
        pltpu.VMEM((chunks, split, block, chunk), BF16),
        pltpu.VMEM((chunks, split, block, chunk), BF16),
        pltpu.VMEM((chunks, split // 2, block, chunk), F32),
        pltpu.VMEM((z_slots, 8, 128), F32),
        pltpu.VMEM((z_slots, 8, 128), F32),
        dma((5,)),
        dma((chunks, split)),
        dma((chunks, split)),
        dma((chunks, split)),
        dma((chunks, split)),
        dma((z_slots,)),
        dma((z_slots,)),
    ]
    if groups > 1:
        scratch += [pltpu.VMEM((groups, most, width), BF16)] * 4 + [dma((groups,))] * 4
    any_spec = pl.BlockSpec(memory_space=pl.ANY)
    vmem_spec = pl.BlockSpec(memory_space=pltpu.VMEM)
    combined, z_loss = pl.pallas_call(
        functools.partial(kernel, cfg),
        out_shape=(
            jax.ShapeDtypeStruct((rows_dev, width), BF16),
            jax.ShapeDtypeStruct((1, 1), F32),
        ),
        in_specs=[any_spec, any_spec, vmem_spec, any_spec, any_spec, any_spec],
        out_specs=(vmem_spec, vmem_spec),
        scratch_shapes=scratch,
        compiler_params=pltpu.CompilerParams(collective_id=0, has_side_effects=True),
    )(token_rows, router_weight, picked, w_gate.T, w_up.T, w_down)
    return combined[None], z_loss.reshape(())


def solution(mesh):
    in_specs = (
        P("dp", "expert", None),
        P(),
        P("dp", None, None),
        P(None, "expert"),
        P(None, "expert"),
        P("expert", None),
    )
    out_specs = (P("dp", "expert", None), P())
    step = functools.partial(body, mesh.shape["expert"], mesh.shape["dp"])
    return jax.shard_map(step, mesh=mesh, in_specs=in_specs, out_specs=out_specs, check_vma=False)
```

```python
import functools

import jax
import jax.numpy as jnp
from jax import lax
from jax.experimental import pallas as pl
from jax.experimental.pallas import tpu as pltpu
from jax.sharding import PartitionSpec as P

MESH = pl.DeviceIdType.MESH
F32 = jnp.float32
BF16 = jnp.bfloat16
LAG = 1


def flip(index, mask):
    result = index
    bit = 0
    while mask >> bit:
        if mask >> bit & 1:
            result = result + 2**bit * (1 - 2 * (index // 2**bit % 2))
        bit += 1
    return result


def times_t(a, b):
    return lax.dot_general(a, b, (((1,), (1,)), ((), ())), preferred_element_type=F32)


def source(j):
    return j - 1 if j % 2 else 0


def kernel(cfg, *refs):
    groups, split, most, dp_bits, ex_bits, chunks, chunk, tokens_all = cfg
    (tok_h, rw_h, chosen_ref, wg_h, wu_h, wd_h, out_ref, z_ref,
     tok, rw, wg, wu, wd, rows_x, send_y, recv_y, part_y, z_acc, z_in,
     local_sem, out_v, out_sem, ag_send, ag_recv, rs_send, rs_recv, z_send, z_recv) = refs[:28]
    me = lax.axis_index("expert")
    me_dp = lax.axis_index("dp")
    my_group = me // split
    rows_dev, width = tok.shape
    cap = chosen_ref.shape[1]
    block = groups * most

    local = [
        pltpu.make_async_copy(src, dst, local_sem.at[i])
        for i, (src, dst) in enumerate(((tok_h, tok), (wg_h, wg), (wu_h, wu), (rw_h, rw), (wd_h, wd)))
    ]
    for copy in local:
        copy.start()

    ex_masks = [1] + list(range(2, split, 2)) + [split * k for k in range(1, groups)]
    partners = [{"expert": flip(me, mask)} for mask in ex_masks]
    partners += [{"dp": flip(me_dp, 1 << b)} for b in range(dp_bits)]
    barrier = pltpu.get_barrier_semaphore()
    for partner in partners:
        pl.semaphore_signal(barrier, inc=1, device_id=partner, device_id_type=MESH)

    t_sub = lax.broadcasted_iota(jnp.int32, (rows_dev, cap), 0)
    sq_row = lax.broadcasted_iota(jnp.int32, (rows_dev, rows_dev), 0)
    sq_col = lax.broadcasted_iota(jnp.int32, (rows_dev, rows_dev), 1)
    before = (sq_row < sq_col).astype(F32).astype(BF16)
    after = (sq_col < sq_row).astype(F32).astype(BF16)
    slot_sub = lax.broadcasted_iota(jnp.int32, (most, rows_dev), 0).astype(F32)
    slot_lane = lax.broadcasted_iota(jnp.int32, (rows_dev, most), 1).astype(F32)
    picks, places, members = [], [], []
    for k in range(groups):
        row = chosen_ref[pl.ds(flip(my_group, k), 1), :] - me * rows_dev
        equal = (row == t_sub).astype(F32)
        member = jnp.max(equal, axis=1, keepdims=True)
        ones = jnp.ones((8, cap), BF16)
        member_row = times_t(ones, equal.astype(BF16))
        rank_row = jnp.dot(member_row.astype(BF16), before, preferred_element_type=F32)
        pick = jnp.where(member_row[0:1] > 0.5, (rank_row[0:1] == slot_sub).astype(F32), 0.0)
        wide = jnp.broadcast_to(member, (rows_dev, most))
        rank_col = jnp.dot(after, wide.astype(BF16), preferred_element_type=F32)
        place = jnp.where(wide > 0.5, (rank_col == slot_lane).astype(F32), 0.0)
        picks.append(pick.astype(BF16))
        places.append(place.astype(BF16))
        members.append(member)

    def cols(c):
        return pl.ds(c * chunk, chunk)

    def ag_copy(c, j):
        return pltpu.make_async_remote_copy(
            src_ref=rows_x.at[c, source(j)],
            dst_ref=rows_x.at[c, j],
            send_sem=ag_send.at[c, j],
            recv_sem=ag_recv.at[c, j],
            device_id={"expert": flip(me, j - source(j))},
            device_id_type=MESH,
        )

    def rs_copy(c, j):
        return pltpu.make_async_remote_copy(
            src_ref=send_y.at[c, j],
            dst_ref=recv_y.at[c, j],
            send_sem=rs_send.at[c, j],
            recv_sem=rs_recv.at[c, j],
            device_id={"expert": flip(me, j - source(j))},
            device_id_type=MESH,
        )

    far = [j for j in range(split - 2, 0, -2)]

    z_steps = [("expert", flip(me, 1 << b)) for b in range(ex_bits)]
    z_steps += [("dp", flip(me_dp, 1 << b)) for b in range(dp_bits)]

    def z_copy(s):
        axis, partner = z_steps[s]
        return pltpu.make_async_remote_copy(
            src_ref=z_acc.at[s],
            dst_ref=z_in.at[s],
            send_sem=z_send.at[s],
            recv_sem=z_recv.at[s],
            device_id={axis: partner},
            device_id_type=MESH,
        )

    def z_advance(s):
        if s > 0:
            z_copy(s - 1).wait()
            z_acc[s] = z_acc[s - 1] + z_in[s - 1]
        if s < len(z_steps):
            z_copy(s).start()

    pl.semaphore_wait(barrier, len(partners))
    local[0].wait()
    if groups == 1:
        for c in range(chunks):
            rows_x[c, 0] = jnp.dot(picks[0], tok[:, cols(c)], preferred_element_type=F32).astype(BF16)
            for j in far:
                ag_copy(c, j).start()
        for c in range(chunks):
            ag_copy(c, 1).start()
    else:
        slots, stage, back_out, back_in, ex_send, ex_recv, bk_send, bk_recv = refs[28:]

        def across(k, src, dst, send, recv):
            return pltpu.make_async_remote_copy(
                src_ref=src.at[k],
                dst_ref=dst.at[k],
                send_sem=send.at[k],
                recv_sem=recv.at[k],
                device_id={"expert": flip(me, split * k)},
                device_id_type=MESH,
            )

        def spread(k):
            sub = lax.broadcasted_iota(jnp.int32, (block, most), 0)
            lane = lax.broadcasted_iota(jnp.int32, (block, most), 1)
            return (sub == lane + k * most).astype(F32).astype(BF16)

        def collect(k):
            sub = lax.broadcasted_iota(jnp.int32, (most, block), 0)
            lane = lax.broadcasted_iota(jnp.int32, (most, block), 1)
            return (lane == sub + k * most).astype(F32).astype(BF16)

        for k in range(groups):
            for c in range(chunks):
                slots[k, :, cols(c)] = jnp.dot(picks[k], tok[:, cols(c)], preferred_element_type=F32).astype(BF16)
            if k:
                across(k, slots, stage, ex_send, ex_recv).start()
        for k in range(1, groups):
            across(k, slots, stage, ex_send, ex_recv).wait()
        for c in range(chunks):
            total = jnp.dot(spread(0), slots[0, :, cols(c)], preferred_element_type=F32)
            for k in range(1, groups):
                total = total + jnp.dot(spread(k), stage[k, :, cols(c)], preferred_element_type=F32)
            rows_x[c, 0] = total.astype(BF16)
            for j in far + [1]:
                ag_copy(c, j).start()

    local[3].wait()
    logits = jnp.dot(tok[...], rw[...], preferred_element_type=F32)
    highest = jnp.max(logits, axis=1, keepdims=True)
    log_total = highest + jnp.log(jnp.sum(jnp.exp(logits - highest), axis=1, keepdims=True))
    z_part = jnp.sum(log_total * log_total, axis=0, keepdims=True)
    z_acc[0] = jnp.broadcast_to(z_part, z_acc.shape[1:])
    lane = lax.broadcasted_iota(jnp.int32, logits.shape, 1)
    window = [
        jnp.sum(jnp.where(lane == flip(my_group, k), logits, 0.0), axis=1, keepdims=True) for k in range(groups)
    ]
    peak = jnp.where(members[0] > 0.5, window[0], -1e30)
    some = members[0]
    for k in range(1, groups):
        peak = jnp.maximum(peak, jnp.where(members[k] > 0.5, window[k], -1e30))
        some = jnp.maximum(some, members[k])
    peak = jnp.where(some > 0.5, peak, 0.0)
    raised = [
        jnp.where(members[k] > 0.5, jnp.exp(jnp.where(members[k] > 0.5, window[k] - peak, -60.0)), 0.0)
        for k in range(groups)
    ]
    denom = functools.reduce(lambda a, b: a + b, raised)
    weights = [value / jnp.where(denom > 0, denom, 1.0) for value in raised]

    local[1].wait()
    local[2].wait()
    gate = jnp.zeros((split * block, wg.shape[0]), F32)
    upper = jnp.zeros((split * block, wg.shape[0]), F32)
    z_done = 0
    for t in range(chunks + LAG):
        if t < chunks:
            for j in reversed(far):
                ag_copy(t, j).wait_recv()
                ag_copy(t, j + 1).start()
        if z_done <= len(z_steps):
            z_advance(z_done)
            z_done += 1
        c = t - LAG
        if c >= 0:
            for j in range(1, split, 2):
                ag_copy(c, j).wait_recv()
            rows = rows_x[c].reshape(split * block, chunk)
            gate = gate + times_t(rows, wg[:, cols(c)])
            upper = upper + times_t(rows, wu[:, cols(c)])
    hidden = (gate / (1.0 + jnp.exp(-gate)) * upper).astype(BF16)

    local[4].wait()

    def down(c):
        part = jnp.dot(hidden, wd[:, cols(c)], preferred_element_type=F32)
        for j in reversed(range(split)):
            piece = part[j * block:(j + 1) * block]
            if j % 2:
                send_y[c, j] = piece.astype(BF16)
                rs_copy(c, j).start()
            else:
                part_y[c, j // 2] = piece

    for c in range(chunks):
        down(c)

    while z_done <= len(z_steps):
        z_advance(z_done)
        z_done += 1
    z_ref[...] = z_acc[len(z_steps)][0:1, 0:1] / tokens_all

    def out_copy(c):
        return pltpu.make_async_copy(out_v.at[:, cols(c)], out_ref.at[:, cols(c)], out_sem.at[c])

    def mix(c, rows_of):
        mixed = weights[0] * jnp.dot(places[0], rows_of(0), preferred_element_type=F32)
        for k in range(1, groups):
            mixed = mixed + weights[k] * jnp.dot(places[k], rows_of(k), preferred_element_type=F32)
        out_v[:, cols(c)] = mixed.astype(out_v.dtype)
        out_copy(c).start()

    for t in range(chunks + LAG):
        if t < chunks:
            for j in far:
                rs_copy(t, j + 1).wait_recv()
                send_y[t, j] = (part_y[t, j // 2] + recv_y[t, j + 1].astype(F32)).astype(BF16)
                rs_copy(t, j).start()
        c = t - LAG
        if c >= 0:
            total = part_y[c, 0]
            for j in [1] + far:
                rs_copy(c, j).wait_recv()
                total = total + recv_y[c, j].astype(F32)
            done = total.astype(BF16)
            if groups == 1:
                mix(c, lambda k: done)
            else:
                send_y[c, 0] = done

    if groups > 1:
        for k in range(groups):
            for c in range(chunks):
                piece = jnp.dot(collect(k), send_y[c, 0], preferred_element_type=F32).astype(BF16)
                back_out[k, :, cols(c)] = piece
            if k:
                across(k, back_out, back_in, bk_send, bk_recv).start()
        for k in range(1, groups):
            across(k, back_out, back_in, bk_send, bk_recv).wait()
        for c in range(chunks):
            mix(c, lambda k: (back_in if k else back_out)[k, :, cols(c)])

    for c in range(chunks):
        for j in range(1, split):
            ag_copy(c, j).wait_send()
            rs_copy(c, j).wait_send()
        out_copy(c).wait()


def body(ex_size, dp_size, tokens, router_weight, chosen, w_gate, w_up, w_down):
    token_rows, picked = tokens[0], chosen[0]
    groups, cap = picked.shape
    rows_dev, width = token_rows.shape
    split = ex_size // groups
    most = 2 * cap // ex_size
    block = groups * most
    ex_bits = ex_size.bit_length() - 1
    dp_bits = dp_size.bit_length() - 1
    chunks = max(1, width // 1024)
    chunk = width // chunks
    cfg = (groups, split, most, dp_bits, ex_bits, chunks, chunk, float(dp_size * ex_size * rows_dev))
    z_slots = ex_bits + dp_bits + 1
    hidden = w_gate.shape[1]
    dma = pltpu.SemaphoreType.DMA
    scratch = [
        pltpu.VMEM((rows_dev, width), BF16),
        pltpu.VMEM(router_weight.shape, BF16),
        pltpu.VMEM((hidden, width), BF16),
        pltpu.VMEM((hidden, width), BF16),
        pltpu.VMEM((hidden, width), BF16),
        pltpu.VMEM((chunks, split, block, chunk), BF16),
        pltpu.VMEM((chunks, split, block, chunk), BF16),
        pltpu.VMEM((chunks, split, block, chunk), BF16),
        pltpu.VMEM((chunks, split // 2, block, chunk), F32),
        pltpu.VMEM((z_slots, 8, 128), F32),
        pltpu.VMEM((z_slots, 8, 128), F32),
        dma((5,)),
        pltpu.VMEM((rows_dev, width), BF16),
        dma((chunks,)),
        dma((chunks, split)),
        dma((chunks, split)),
        dma((chunks, split)),
        dma((chunks, split)),
        dma((z_slots,)),
        dma((z_slots,)),
    ]
    if groups > 1:
        scratch += [pltpu.VMEM((groups, most, width), BF16)] * 4 + [dma((groups,))] * 4
    any_spec = pl.BlockSpec(memory_space=pl.ANY)
    vmem_spec = pl.BlockSpec(memory_space=pltpu.VMEM)
    combined, z_loss = pl.pallas_call(
        functools.partial(kernel, cfg),
        out_shape=(
            jax.ShapeDtypeStruct((rows_dev, width), BF16),
            jax.ShapeDtypeStruct((1, 1), F32),
        ),
        in_specs=[any_spec, any_spec, vmem_spec, any_spec, any_spec, any_spec],
        out_specs=(any_spec, vmem_spec),
        scratch_shapes=scratch,
        compiler_params=pltpu.CompilerParams(collective_id=0, has_side_effects=True),
    )(token_rows, router_weight, picked, w_gate.T, w_up.T, w_down)
    return combined[None], z_loss.reshape(())


def solution(mesh):
    in_specs = (
        P("dp", "expert", None),
        P(),
        P("dp", None, None),
        P(None, "expert"),
        P(None, "expert"),
        P("expert", None),
    )
    out_specs = (P("dp", "expert", None), P())
    step = functools.partial(body, mesh.shape["expert"], mesh.shape["dp"])
    return jax.shard_map(step, mesh=mesh, in_specs=in_specs, out_specs=out_specs, check_vma=False)
```
